512 devices in a mesh: rep: 64 (over z, y_lo, core), fsdp: 8 (over y_hi, x).
Axes of the slice: x: 4, y: 4 (y_hi: 2, y_lo: 2; y = y_hi * 2 + y_lo), z: 16, core: 2. Of those that a mesh axis runs over, the one named last changes fastest.
Arguments:
- tokens: bfloat16 [131072, 4096], P(('rep', 'fsdp')), may hold values from -6 to 6
- weights: float32 [64, 4096, 512], P('rep', 'fsdp'), may hold values from -6 to 6
- verdict_head: bfloat16 [512, 128], replicated
- verdict: int32 [131072], P(('rep', 'fsdp')), may hold values from 0 to 127
- step_index: int32 [1], replicated, may hold values from 0 to 999
Outputs:
- mixed_weights: float32 [64, 4096, 512], P('rep', 'fsdp')
- token_loss: float32 [131072], P(('rep', 'fsdp'))
The draws below stay inside these ranges and needn't reach their ends.
All inputs are finite; a program needn't handle non-finite values.
Results may differ from the reference program's by a relative error of at most 0.012.
The reference program's roundings to bfloat16 on the way count: a program that leaves them out, or rounds other values in their place, can miss the bound.
Values may be sent and summed in bfloat16 or wider, within the bound.
A program may use at most 64 MiB of HBM per device.

```python
import jax
import jax.numpy as jnp
from jax import lax

D = 4096
KV = 512
GRADES = 128
TOK_DEV = 256
TOKENS = 131072
N_REP = 64
N_FSDP = 8


def draw_verdict_head(key, part):
    base_key = jax.random.fold_in(key, 11)
    scale_key = jax.random.fold_in(key, 12)
    base = jax.random.truncated_normal(base_key, -4.0, 4.0, (KV, GRADES), jnp.float32)
    column_scale = jnp.exp(jax.random.uniform(scale_key, (1, GRADES), jnp.float32, 0.0, 1.0))
    entries = base * column_scale * KV ** (-0.5)
    return entries.astype(jnp.bfloat16)


def set_ends(drawn, own_key, smallest, high):
    spot = [jax.random.randint(jax.random.fold_in(own_key, axis), (), 0, length) for axis, length in enumerate(drawn.shape)]
    widest = drawn.shape.index(max(drawn.shape))
    neighbour = spot[:widest] + [(spot[widest] + 1) % drawn.shape[widest]] + spot[widest + 1:]
    return drawn.at[tuple(spot)].set(smallest).at[tuple(neighbour)].set(high)


def steps_of(own_key, shape, cuts, low, top_value):
    gain, own = 1.0, jax.random.fold_in(own_key, 6)
    for axis_at, shards_of in cuts:
        draws = jnp.exp(jax.random.uniform(jax.random.fold_in(own, axis_at), (shards_of,), jnp.float32, low / len(cuts), top_value / len(cuts)))
        gain = gain * jnp.repeat(draws, shape[axis_at] // shards_of).reshape([-1 if axis == axis_at else 1 for axis in range(len(shape))])
    return gain


def noise(stream_key, extent, scale, bound, split=(), held_as=jnp.bfloat16):
    drawn = scale * jax.random.normal(stream_key, extent, jnp.float32)
    if split:
        drawn = drawn * steps_of(stream_key, extent, split, -0.22, 0.18)
    return jnp.clip(drawn, -bound, bound).astype(held_as)


def setup_inputs(seed: int = 0) -> dict:
    keys = jax.random.split(jax.random.key(seed), 6)
    tokens = noise(keys[0], (TOKENS, D), 1.0, 6.0, ((0, 512),))
    weights = noise(keys[1], (N_REP, D, KV), 1.0, 6.0, ((0, 64), (1, 8)), jnp.float32)
    verdict_head = draw_verdict_head(jax.random.fold_in(keys[5], 71), 0)
    verdict = set_ends(jax.random.randint(keys[3], (TOKENS,), 0, GRADES), jax.random.fold_in(keys[3], 1), 0, GRADES - 1).astype(jnp.int32)
    step_index = jax.random.randint(keys[4], (1,), 0, 1000).astype(jnp.int32)
    return dict(tokens=tokens, weights=weights, verdict_head=verdict_head, verdict=verdict, step_index=step_index)


eps_value = 1e-06
step_size = 8.0

def head_gradient(values, verdict, verdict_head, inv_root):
    mean_square = lax.optimization_barrier(jnp.mean(values * values, axis=-1, keepdims=True))
    recip = lax.rsqrt(mean_square + eps_value)
    normed = values * recip
    logits = jnp.dot(normed.astype(jnp.bfloat16), verdict_head, preferred_element_type=jnp.float32)
    total = jax.nn.logsumexp(logits, axis=-1)
    labels = jnp.arange(logits.shape[1], dtype=jnp.int32)[None, :] == verdict[:, None]
    chosen = lax.optimization_barrier(jnp.sum(jnp.where(labels, logits, jnp.zeros_like(logits)), axis=-1))
    token_loss = total - chosen
    dlogits = (jax.nn.softmax(logits, axis=-1) - labels.astype(logits.dtype)).astype(jnp.bfloat16)
    along = jnp.dot(dlogits, verdict_head.T, preferred_element_type=jnp.float32)
    projected = lax.optimization_barrier(jnp.mean(normed * along, axis=-1, keepdims=True))
    grad_values = ((along - normed * projected) * recip * inv_root).astype(jnp.bfloat16)
    return (token_loss, grad_values)

def reference(tokens, weights, verdict_head, verdict, step_index):
    inv_root = D ** (-0.5)
    rep_tokens = tokens.reshape(N_REP, N_FSDP * TOK_DEV, D)
    rep_verdict = verdict.reshape(N_REP, N_FSDP * TOK_DEV)

    def replica_step(packed):
        features, master, targets = packed
        values = jnp.dot(features, master.astype(jnp.bfloat16), preferred_element_type=jnp.float32) * inv_root
        token_loss, grad_values = head_gradient(values, targets, verdict_head, inv_root)
        blocks_in = features.reshape(N_FSDP, TOK_DEV, D).astype(jnp.float32)
        blocks_grad = grad_values.reshape(N_FSDP, TOK_DEV, KV).astype(jnp.float32)
        terms = jnp.einsum('btd,btk->bdk', blocks_in, blocks_grad)
        rounded = lax.optimization_barrier(terms.astype(jnp.bfloat16))
        grad = lax.optimization_barrier(jnp.sum(rounded.astype(jnp.float32), axis=0))
        return (master - step_size * grad, token_loss)
    updated, token_loss = lax.map(replica_step, (rep_tokens, weights, rep_verdict))
    levels = N_REP.bit_length() - 1
    level_index = (step_index[0] % levels).astype(jnp.int32)
    distance = jnp.left_shift(jnp.int32(1), level_index)
    mixed_weights = 0.5 * (updated + jnp.roll(updated, distance, axis=0))
    return (mixed_weights, token_loss.reshape(-1))
```

```python
import functools

import jax
import jax.numpy as jnp
from jax import lax
from jax.experimental import pallas as pl
from jax.experimental.pallas import tpu as pltpu
from jax.sharding import PartitionSpec as P

MESH = pl.DeviceIdType.MESH
EPS = 1e-06
STEP = 8.0
NX = 4
CHUNKS = 4


def tdot(a, b):
    return lax.dot_general(a, b, (((0,), (0,)), ((), ())), preferred_element_type=jnp.float32)


def kernel(inv_root, tok_hbm, w_hbm, head_ref, verdict_ref, upd_ref, half_ref, loss_ref,
           tok, tok_y, wv, wall, acc, labels, psend, precv, gsend, grecv, own, opp, sides,
           opp_in, side_in, local_sem, tok_ss, tok_rs, w_ss, w_rs, p_ss, p_rs, g_ss, g_rs,
           o_ss, o_rs, s_ss, s_rs):
    rep, me = lax.axis_index("rep"), lax.axis_index("fsdp")
    row, x = me // NX, me % NX
    pair = (1 - row) * NX + x
    xs = [row * NX + (x + 1) % NX, row * NX + (x + NX - 1) % NX]
    depth, kv = wv.shape
    half = depth // 2
    rows = tok.shape[0]
    wide = NX * depth
    part = rows // CHUNKS

    def remote(src, dst, ss, rs, peer):
        return pltpu.make_async_remote_copy(src_ref=src, dst_ref=dst, send_sem=ss, recv_sem=rs,
                                            device_id=(rep, peer), device_id_type=MESH)

    def block(of):
        return pl.multiple_of(((x + of + NX) % NX) * depth, depth)

    w_in = pltpu.make_async_copy(w_hbm, wv, local_sem.at[0])
    w_in.start()
    t_in = pltpu.make_async_copy(tok_hbm.at[:, pl.ds(pl.multiple_of(row * wide, wide), wide)], tok,
                                 local_sem.at[1])
    t_in.start()
    barrier = pltpu.get_barrier_semaphore()
    for peer in xs + [pair]:
        pl.semaphore_signal(barrier, inc=1, device_id=(rep, peer), device_id_type=MESH)
    w_in.wait()
    wall[pl.ds(block(0), depth), :] = wv[...].astype(jnp.bfloat16)
    pl.semaphore_wait(barrier, 3)

    tok_out = []
    for c in range(CHUNKS):
        copy = remote(
            tok_hbm.at[pl.ds(c * part, part), pl.ds(pl.multiple_of((1 - row) * wide, wide), wide)],
            tok_y.at[pl.ds(c * part, part), :], tok_ss.at[c], tok_rs.at[c], pair)
        tok_out.append(copy)

    def w_copy(d, stage):
        hop = d if stage in (0, 2) else 1 - d
        of = 0 if stage < 2 else (-1 if d == 0 else 1)
        where = pl.ds(pl.multiple_of(block(of) + hop * half, half), half)
        return remote(wall.at[where, :], wall.at[where, :], w_ss.at[d, stage], w_rs.at[d, stage], xs[d])

    w_out = [[w_copy(d, s) for s in range(3)] for d in range(2)]
    for d in range(2):
        w_out[d][0].start()
    for copy in tok_out:
        copy.start()
    for d in range(2):
        w_out[d][1].start()

    hit = lax.broadcasted_iota(jnp.int32, (labels.shape[1], rows), 0) == verdict_ref[...]
    labels[...] = jnp.transpose(hit.astype(jnp.float32))
    t_in.wait()

    def product(of):
        return jnp.dot(tok[:, pl.ds(block(of), depth)], wall[pl.ds(block(of), depth), :],
                       preferred_element_type=jnp.float32)

    acc[...] = product(0)
    for d in range(2):
        w_out[d][0].wait_recv()
        w_out[d][2].start()
    for d in range(2):
        w_out[d][1].wait_recv()
    acc[...] += product(-1) + product(1)
    for d in range(2):
        w_out[d][2].wait_recv()
    acc[...] += product(2)

    p_out = []
    for c in range(CHUNKS):
        here = pl.ds(c * part, part)
        tok_out[c].wait_recv()
        psend[here, :] = jnp.dot(tok_y[here, :], wall[...],
                                 preferred_element_type=jnp.float32).astype(jnp.bfloat16)
        copy = remote(psend.at[here, :], precv.at[here, :], p_ss.at[c], p_rs.at[c], pair)
        copy.start()
        p_out.append(copy)
    for copy in p_out:
        copy.wait_recv()

    values = (acc[...] + precv[...].astype(jnp.float32)) * inv_root
    recip = lax.rsqrt(jnp.mean(values * values, axis=-1, keepdims=True) + EPS)
    normed = values * recip
    logits = jnp.dot(normed.astype(jnp.bfloat16), head_ref[...], preferred_element_type=jnp.float32)
    top = jnp.max(logits, axis=-1, keepdims=True)
    powers = jnp.exp(logits - top)
    total = jnp.sum(powers, axis=-1, keepdims=True)
    chosen = jnp.sum(logits * labels[...], axis=-1, keepdims=True)
    dlogits = (powers / total - labels[...]).astype(jnp.bfloat16)
    along = lax.dot_general(dlogits, head_ref[...], (((1,), (1,)), ((), ())),
                            preferred_element_type=jnp.float32)
    projected = jnp.mean(normed * along, axis=-1, keepdims=True)
    gsend[...] = ((along - normed * projected) * recip * inv_root).astype(jnp.bfloat16)
    g_out = remote(gsend, grecv, g_ss.at[0], g_rs.at[0], pair)
    g_out.start()
    loss = jnp.log(total) + top - chosen
    loss_ref[...] = jnp.transpose(jnp.broadcast_to(loss, (rows, 128)))[0:1, :]

    for k, of in enumerate((2, 1, -1, 0)):
        own[k] = tdot(tok[:, pl.ds(block(of), depth)], gsend[...]).astype(jnp.bfloat16)
    g_out.wait_recv()

    def summed(k, of):
        other = tdot(tok_y[:, pl.ds(block(of), depth)], grecv[...]).astype(jnp.bfloat16)
        return own[k].astype(jnp.float32) + other.astype(jnp.float32)

    opp[...] = summed(0, 2).astype(jnp.bfloat16)
    o_out = []
    for d in range(2):
        copy = remote(opp.at[pl.ds(d * half, half), :], opp_in.at[d], o_ss.at[d], o_rs.at[d], xs[d])
        copy.start()
        o_out.append(copy)
    s_out = [[None, None], [None, None]]
    for d in range(2):
        sides[d] = summed(1 + d, 1 - 2 * d).astype(jnp.bfloat16)
        for h in range(2):
            at = pl.ds(h * half, half)
            s_out[d][h] = remote(sides.at[d, at, :], side_in.at[d, at, :], s_ss.at[d, h], s_rs.at[d, h], xs[d])
        s_out[d][1 - d].start()
    for d in range(2):
        at = pl.ds(d * half, half)
        o_out[d].wait_recv()
        sides[d, at, :] = (sides[d, at, :].astype(jnp.float32)
                           + opp_in[d].astype(jnp.float32)).astype(jnp.bfloat16)
        s_out[d][d].start()
    acc2 = upd_ref
    acc2[...] = summed(3, 0)
    for d in range(2):
        for h in range(2):
            s_out[d][h].wait_recv()
    grad = acc2[...] + side_in[0].astype(jnp.float32) + side_in[1].astype(jnp.float32)
    updated = wv[...] - STEP * grad
    upd_ref[...] = updated
    half_ref[...] = updated.astype(jnp.bfloat16)
    for copy in tok_out + w_out[0] + w_out[1] + p_out + [g_out] + o_out + s_out[0] + s_out[1]:
        copy.wait_send()


def step_call(tokens, weights, head, verdict):
    rows, wide = tokens.shape
    depth, kv = weights.shape
    grades = head.shape[1]
    any_spec = pl.BlockSpec(memory_space=pl.ANY)
    vmem = pl.BlockSpec(memory_space=pltpu.VMEM)
    bf16, f32 = jnp.bfloat16, jnp.float32
    sem = pltpu.SemaphoreType.DMA
    return pl.pallas_call(
        functools.partial(kernel, wide ** (-0.5)),
        out_shape=(jax.ShapeDtypeStruct((depth, kv), f32), jax.ShapeDtypeStruct((depth, kv), bf16),
                   jax.ShapeDtypeStruct((1, rows), f32)),
        in_specs=[any_spec, any_spec, vmem, vmem],
        out_specs=(vmem, vmem, vmem),
        scratch_shapes=[
            pltpu.VMEM((rows, NX * depth), bf16), pltpu.VMEM((rows, NX * depth), bf16),
            pltpu.VMEM((depth, kv), f32), pltpu.VMEM((NX * depth, kv), bf16),
            pltpu.VMEM((rows, kv), f32), pltpu.VMEM((rows, grades), f32),
            pltpu.VMEM((rows, kv), bf16), pltpu.VMEM((rows, kv), bf16),
            pltpu.VMEM((rows, kv), bf16), pltpu.VMEM((rows, kv), bf16),
            pltpu.VMEM((NX, depth, kv), bf16), pltpu.VMEM((depth, kv), bf16),
            pltpu.VMEM((2, depth, kv), bf16), pltpu.VMEM((2, depth // 2, kv), bf16),
            pltpu.VMEM((2, depth, kv), bf16),
            sem((2,)), sem((CHUNKS,)), sem((CHUNKS,)), sem((2, 3)), sem((2, 3)),
            sem((CHUNKS,)), sem((CHUNKS,)), sem((1,)), sem((1,)), sem((2,)), sem((2,)),
            sem((2, 2)), sem((2, 2)),
        ],
        compiler_params=pltpu.CompilerParams(collective_id=0, has_side_effects=True,
                                             vmem_limit_bytes=48 << 20),
        name="step",
    )(tokens, weights, head, verdict)


def from_behind(value, distance):
    n = lax.axis_size("rep")
    return lax.ppermute(value, "rep", [((i - distance) % n, i) for i in range(n)])


def local(tokens, weights, verdict_head, verdict, step_index):
    levels = lax.axis_size("rep").bit_length() - 1
    level = step_index[0] % levels
    updated, sent, loss = step_call(tokens, weights[0], verdict_head, verdict[None, :])
    received = lax.switch(level, [functools.partial(from_behind, distance=1 << lv) for lv in range(levels)], sent)
    mixed = 0.5 * (updated + received.astype(jnp.float32))
    return mixed[None], loss.reshape(-1)


def solution(mesh):
    return jax.shard_map(
        local,
        mesh=mesh,
        in_specs=(P(("rep", "fsdp"), None), P("rep", "fsdp", None), P(), P(("rep", "fsdp")), P()),
        out_specs=(P("rep", "fsdp", None), P(("rep", "fsdp"))),
        check_vma=False,
    )
```

```python
import functools

import jax
import jax.numpy as jnp
from jax import lax
from jax.experimental import pallas as pl
from jax.experimental.pallas import tpu as pltpu
from jax.sharding import PartitionSpec as P

MESH = pl.DeviceIdType.MESH
EPS = 1e-06
STEP = 8.0
NX = 4
CHUNKS = 4
SLABS = 2
VMEM_BYTES = 64000 << 10


def tdot(a, b):
    return lax.dot_general(a, b, (((0,), (0,)), ((), ())), preferred_element_type=jnp.float32)


def kernel(inv_root, distance, tok_hbm, w_hbm, head_ref, verdict_ref, mixed_ref, loss_ref,
           tok, tok_y, wv, wall, acc, labels, psend, precv, gsend, grecv, own, mine, opp, sides,
           opp_in, side_in, mix_out, mix_in, local_sem, tok_ss, tok_rs, w_ss, w_rs, p_ss, p_rs,
           g_ss, g_rs, o_ss, o_rs, s_ss, s_rs, m_ss, m_rs):
    rep, me = lax.axis_index("rep"), lax.axis_index("fsdp")
    row, x = me // NX, me % NX
    pair = (1 - row) * NX + x
    xs = [row * NX + (x + 1) % NX, row * NX + (x + NX - 1) % NX]
    depth, kv = wv.shape
    half = depth // 2
    rows = tok.shape[0]
    wide = NX * depth
    part = rows // CHUNKS

    n_rep = lax.axis_size("rep")
    ahead, behind = (rep + distance) % n_rep, (rep + n_rep - distance) % n_rep
    cols = kv // SLABS

    def remote(src, dst, ss, rs, peer, of_rep=None):
        return pltpu.make_async_remote_copy(src_ref=src, dst_ref=dst, send_sem=ss, recv_sem=rs,
                                            device_id=(rep if of_rep is None else of_rep, peer),
                                            device_id_type=MESH)

    def block(of):
        return pl.multiple_of(((x + of + NX) % NX) * depth, depth)

    w_in = pltpu.make_async_copy(w_hbm, wv, local_sem.at[0])
    w_in.start()
    t_in = pltpu.make_async_copy(tok_hbm.at[:, pl.ds(pl.multiple_of(row * wide, wide), wide)], tok,
                                 local_sem.at[1])
    t_in.start()
    barrier = pltpu.get_barrier_semaphore()
    for peer in xs + [pair]:
        pl.semaphore_signal(barrier, inc=1, device_id=(rep, peer), device_id_type=MESH)
    pl.semaphore_signal(barrier, inc=1, device_id=(behind, me), device_id_type=MESH)
    w_in.wait()
    wall[pl.ds(block(0), depth), :] = wv[...].astype(jnp.bfloat16)
    pl.semaphore_wait(barrier, 4)

    tok_out = []
    for c in range(CHUNKS):
        copy = remote(
            tok_hbm.at[pl.ds(c * part, part), pl.ds(pl.multiple_of((1 - row) * wide, wide), wide)],
            tok_y.at[pl.ds(c * part, part), :], tok_ss.at[c], tok_rs.at[c], pair)
        tok_out.append(copy)

    def w_copy(d, stage):
        hop = d if stage in (0, 2) else 1 - d
        of = 0 if stage < 2 else (-1 if d == 0 else 1)
        where = pl.ds(pl.multiple_of(block(of) + hop * half, half), half)
        return remote(wall.at[where, :], wall.at[where, :], w_ss.at[d, stage], w_rs.at[d, stage], xs[d])

    w_out = [[w_copy(d, s) for s in range(3)] for d in range(2)]
    for d in range(2):
        w_out[d][0].start()
    for copy in tok_out:
        copy.start()
    for d in range(2):
        w_out[d][1].start()

    hit = lax.broadcasted_iota(jnp.int32, (labels.shape[1], rows), 0) == verdict_ref[...]
    labels[...] = jnp.transpose(hit.astype(jnp.float32))
    t_in.wait()

    def product(of):
        return jnp.dot(tok[:, pl.ds(block(of), depth)], wall[pl.ds(block(of), depth), :],
                       preferred_element_type=jnp.float32)

    acc[...] = product(0)
    for d in range(2):
        w_out[d][0].wait_recv()
        w_out[d][2].start()
    for d in range(2):
        w_out[d][1].wait_recv()
    acc[...] += product(-1) + product(1)
    for d in range(2):
        w_out[d][2].wait_recv()
    acc[...] += product(2)

    p_out = []
    for c in range(CHUNKS):
        here = pl.ds(c * part, part)
        tok_out[c].wait_recv()
        psend[here, :] = jnp.dot(tok_y[here, :], wall[...],
                                 preferred_element_type=jnp.float32).astype(jnp.bfloat16)
        copy = remote(psend.at[here, :], precv.at[here, :], p_ss.at[c], p_rs.at[c], pair)
        copy.start()
        p_out.append(copy)
    for copy in p_out:
        copy.wait_recv()

    values = (acc[...] + precv[...].astype(jnp.float32)) * inv_root
    recip = lax.rsqrt(jnp.mean(values * values, axis=-1, keepdims=True) + EPS)
    normed = values * recip
    logits = jnp.dot(normed.astype(jnp.bfloat16), head_ref[...], preferred_element_type=jnp.float32)
    top = jnp.max(logits, axis=-1, keepdims=True)
    powers = jnp.exp(logits - top)
    total = jnp.sum(powers, axis=-1, keepdims=True)
    chosen = jnp.sum(logits * labels[...], axis=-1, keepdims=True)
    dlogits = (powers / total - labels[...]).astype(jnp.bfloat16)
    along = lax.dot_general(dlogits, head_ref[...], (((1,), (1,)), ((), ())),
                            preferred_element_type=jnp.float32)
    projected = jnp.mean(normed * along, axis=-1, keepdims=True)
    grad_values = ((along - normed * projected) * recip * inv_root).astype(jnp.bfloat16)
    g_out = []
    for q in range(SLABS):
        gsend[q] = grad_values[:, q * cols:(q + 1) * cols]
        copy = remote(gsend.at[q], grecv.at[q], g_ss.at[q], g_rs.at[q], pair)
        copy.start()
        g_out.append(copy)
    loss = jnp.log(total) + top - chosen
    loss_ref[...] = jnp.transpose(jnp.broadcast_to(loss, (rows, 128)))[0:1, :]

    for q in range(SLABS):
        for k, of in enumerate((2, 1, -1, 0)):
            own[q, k] = tdot(tok[:, pl.ds(block(of), depth)], gsend[q]).astype(jnp.bfloat16)

    def summed(q, k, of):
        other = tdot(tok_y[:, pl.ds(block(of), depth)], grecv[q]).astype(jnp.bfloat16)
        return own[q, k].astype(jnp.float32) + other.astype(jnp.float32)

    def half_at(h):
        return pl.ds(h * half, half)

    def opp_copy(q, d):
        return remote(opp.at[q, half_at(d), :], opp_in.at[q, d], o_ss.at[q, d], o_rs.at[q, d], xs[d])

    def side_copy(q, d, h):
        return remote(sides.at[q, d, half_at(h), :], side_in.at[q, d, half_at(h), :],
                      s_ss.at[q, d, h], s_rs.at[q, d, h], xs[d])

    def send_opposite(q):
        g_out[q].wait_recv()
        opp[q] = summed(q, 0, 2).astype(jnp.bfloat16)
        for d in range(2):
            opp_copy(q, d).start()

    def send_plain(q):
        for d in range(2):
            sides[q, d] = summed(q, 1 + d, 1 - 2 * d).astype(jnp.bfloat16)
            side_copy(q, d, 1 - d).start()

    def send_added(q):
        for d in range(2):
            opp_copy(q, d).wait_recv()
            sides[q, d, half_at(d), :] = (sides[q, d, half_at(d), :].astype(jnp.float32)
                                          + opp_in[q, d].astype(jnp.float32)).astype(jnp.bfloat16)
            side_copy(q, d, d).start()

    def mix_copy(q):
        return remote(mix_out.at[q], mix_in.at[q], m_ss.at[q], m_rs.at[q], me, ahead)

    def send_updated(q):
        for d in range(2):
            for h in range(2):
                side_copy(q, d, h).wait_recv()
        grad = mine[q] + side_in[q, 0].astype(jnp.float32) + side_in[q, 1].astype(jnp.float32)
        updated = wv[:, q * cols:(q + 1) * cols] - STEP * grad
        mix_out[q] = updated.astype(jnp.bfloat16)
        mix_copy(q).start()
        mine[q] = updated

    for q in range(SLABS):
        send_opposite(q)
        if q:
            send_added(q - 1)
        send_plain(q)
        mine[q] = summed(q, 3, 0)
    send_added(SLABS - 1)
    for q in range(SLABS):
        send_updated(q)
    for q in range(SLABS):
        mix_copy(q).wait_recv()
        mixed_ref[:, q * cols:(q + 1) * cols] = 0.5 * (mine[q] + mix_in[q].astype(jnp.float32))
    for copy in tok_out + w_out[0] + w_out[1] + p_out + g_out:
        copy.wait_send()
    for q in range(SLABS):
        for d in range(2):
            opp_copy(q, d).wait_send()
            for h in range(2):
                side_copy(q, d, h).wait_send()
        mix_copy(q).wait_send()


def step_call(level, tokens, weights, head, verdict):
    rows, wide = tokens.shape
    depth, kv = weights.shape
    grades = head.shape[1]
    cols = kv // SLABS
    any_spec = pl.BlockSpec(memory_space=pl.ANY)
    vmem = pl.BlockSpec(memory_space=pltpu.VMEM)
    bf16, f32 = jnp.bfloat16, jnp.float32
    sem = pltpu.SemaphoreType.DMA
    return pl.pallas_call(
        functools.partial(kernel, wide ** (-0.5), 1 << level),
        out_shape=(jax.ShapeDtypeStruct((depth, kv), f32), jax.ShapeDtypeStruct((1, rows), f32)),
        in_specs=[any_spec, any_spec, vmem, vmem],
        out_specs=(vmem, vmem),
        scratch_shapes=[
            pltpu.VMEM((rows, NX * depth), bf16), pltpu.VMEM((rows, NX * depth), bf16),
            pltpu.VMEM((depth, kv), f32), pltpu.VMEM((NX * depth, kv), bf16),
            pltpu.VMEM((rows, kv), f32), pltpu.VMEM((rows, grades), f32),
            pltpu.VMEM((rows, kv), bf16), pltpu.VMEM((rows, kv), bf16),
            pltpu.VMEM((SLABS, rows, cols), bf16), pltpu.VMEM((SLABS, rows, cols), bf16),
            pltpu.VMEM((SLABS, NX, depth, cols), bf16), pltpu.VMEM((SLABS, depth, cols), f32),
            pltpu.VMEM((SLABS, depth, cols), bf16), pltpu.VMEM((SLABS, 2, depth, cols), bf16),
            pltpu.VMEM((SLABS, 2, depth // 2, cols), bf16), pltpu.VMEM((SLABS, 2, depth, cols), bf16),
            pltpu.VMEM((SLABS, depth, cols), bf16), pltpu.VMEM((SLABS, depth, cols), bf16),
            sem((2,)), sem((CHUNKS,)), sem((CHUNKS,)), sem((2, 3)), sem((2, 3)),
            sem((CHUNKS,)), sem((CHUNKS,)), sem((SLABS,)), sem((SLABS,)),
            sem((SLABS, 2)), sem((SLABS, 2)), sem((SLABS, 2, 2)), sem((SLABS, 2, 2)),
            sem((SLABS,)), sem((SLABS,)),
        ],
        compiler_params=pltpu.CompilerParams(collective_id=level, has_side_effects=True,
                                             vmem_limit_bytes=VMEM_BYTES),
        name="step",
    )(tokens, weights, head, verdict)


def local(tokens, weights, verdict_head, verdict, step_index):
    levels = lax.axis_size("rep").bit_length() - 1
    level = step_index[0] % levels
    mixed, loss = lax.switch(
        level, [functools.partial(step_call, lv) for lv in range(levels)],
        tokens, weights[0], verdict_head, verdict[None, :])
    return mixed[None], loss.reshape(-1)


def solution(mesh):
    return jax.shard_map(
        local,
        mesh=mesh,
        in_specs=(P(("rep", "fsdp"), None), P("rep", "fsdp", None), P(), P(("rep", "fsdp")), P()),
        out_specs=(P("rep", "fsdp", None), P(("rep", "fsdp"))),
        check_vma=False,
    )
```

```python
import functools

import jax
import jax.numpy as jnp
from jax import lax
from jax.experimental import pallas as pl
from jax.experimental.pallas import tpu as pltpu
from jax.sharding import PartitionSpec as P

MESH = pl.DeviceIdType.MESH
EPS = 1e-06
STEP = 8.0
NX = 4
CHUNKS = 4
SLABS = 2
VMEM_BYTES = 64000 << 10


def tdot(a, b):
    return lax.dot_general(a, b, (((0,), (0,)), ((), ())), preferred_element_type=jnp.float32)


def kernel(inv_root, distance, tok_hbm, w_hbm, head_ref, verdict_ref, mixed_ref, loss_ref,
           tok, tok_y, wv, wall, acc, labels, psend, precv, gsend, grecv, own, mine, opp, sides,
           opp_in, side_in, mix_out, mix_in, tok_x, grad_x, terms, term_out, term_in, local_sem, tok_ss, tok_rs, w_ss, w_rs, p_ss, p_rs,
           g_ss, g_rs, o_ss, o_rs, s_ss, s_rs, m_ss, m_rs, tx_ss, tx_rs, gx_ss, gx_rs, r_ss, r_rs):
    rep, me = lax.axis_index("rep"), lax.axis_index("fsdp")
    row, x = me // NX, me % NX
    pair = (1 - row) * NX + x
    xs = [row * NX + (x + 1) % NX, row * NX + (x + NX - 1) % NX]
    turns = {j: row * NX + (x + j) % NX for j in (1, 3, 2)}
    depth, kv = wv.shape
    half = depth // 2
    rows = tok.shape[0]
    wide = NX * depth
    part = rows // CHUNKS

    n_rep = lax.axis_size("rep")
    ahead, behind = (rep + distance) % n_rep, (rep + n_rep - distance) % n_rep
    cols = kv // SLABS

    def remote(src, dst, ss, rs, peer, of_rep=None):
        return pltpu.make_async_remote_copy(src_ref=src, dst_ref=dst, send_sem=ss, recv_sem=rs,
                                            device_id=(rep if of_rep is None else of_rep, peer),
                                            device_id_type=MESH)

    def block(of):
        return pl.multiple_of(((x + of + NX) % NX) * depth, depth)

    w_in = pltpu.make_async_copy(w_hbm, wv, local_sem.at[0])
    w_in.start()
    t_in = pltpu.make_async_copy(tok_hbm.at[:, pl.ds(pl.multiple_of(row * wide, wide), wide)], tok,
                                 local_sem.at[1])
    t_in.start()
    x_in = []
    for k in range(2):
        at = pl.multiple_of(((row + k) % 2 * NX + x) * depth, depth)
        x_in.append(pltpu.make_async_copy(tok_hbm.at[:, pl.ds(at, depth)], tok_x.at[0, k], local_sem.at[2 + k]))
        x_in[k].start()
    barrier = pltpu.get_barrier_semaphore()
    for peer in list(turns.values()) + [pair]:
        pl.semaphore_signal(barrier, inc=1, device_id=(rep, peer), device_id_type=MESH)
    pl.semaphore_signal(barrier, inc=1, device_id=(behind, me), device_id_type=MESH)
    w_in.wait()
    wall[pl.ds(block(0), depth), :] = wv[...].astype(jnp.bfloat16)
    pl.semaphore_wait(barrier, 5)

    tok_out = []
    for c in range(CHUNKS):
        copy = remote(
            tok_hbm.at[pl.ds(c * part, part), pl.ds(pl.multiple_of((1 - row) * wide, wide), wide)],
            tok_y.at[pl.ds(c * part, part), :], tok_ss.at[c], tok_rs.at[c], pair)
        tok_out.append(copy)

    def w_copy(d, stage):
        hop = d if stage in (0, 2) else 1 - d
        of = 0 if stage < 2 else (-1 if d == 0 else 1)
        where = pl.ds(pl.multiple_of(block(of) + hop * half, half), half)
        return remote(wall.at[where, :], wall.at[where, :], w_ss.at[d, stage], w_rs.at[d, stage], xs[d])

    w_out = [[w_copy(d, s) for s in range(3)] for d in range(2)]
    for d in range(2):
        w_out[d][0].start()
    for copy in tok_out:
        copy.start()
    for d in range(2):
        w_out[d][1].start()

    hit = lax.broadcasted_iota(jnp.int32, (labels.shape[1], rows), 0) == verdict_ref[...]
    labels[...] = jnp.transpose(hit.astype(jnp.float32))
    t_in.wait()

    def product(of):
        return jnp.dot(tok[:, pl.ds(block(of), depth)], wall[pl.ds(block(of), depth), :],
                       preferred_element_type=jnp.float32)

    acc[...] = product(0)
    for d in range(2):
        w_out[d][0].wait_recv()
        w_out[d][2].start()
    x_out = []
    for j, peer in turns.items():
        for k in range(2):
            at = pl.multiple_of(((row + k) % 2 * NX + (x + j) % NX) * depth, depth)
            copy = remote(tok_hbm.at[:, pl.ds(at, depth)], tok_x.at[j, k], tx_ss.at[j, k], tx_rs.at[j, k], peer)
            copy.start()
            x_out.append(copy)
    for d in range(2):
        w_out[d][1].wait_recv()
    acc[...] += product(-1) + product(1)
    for d in range(2):
        w_out[d][2].wait_recv()
    acc[...] += product(2)

    p_out = []
    for c in range(CHUNKS):
        here = pl.ds(c * part, part)
        tok_out[c].wait_recv()
        psend[here, :] = jnp.dot(tok_y[here, :], wall[...],
                                 preferred_element_type=jnp.float32).astype(jnp.bfloat16)
        copy = remote(psend.at[here, :], precv.at[here, :], p_ss.at[c], p_rs.at[c], pair)
        copy.start()
        p_out.append(copy)
    for copy in p_out:
        copy.wait_recv()

    values = (acc[...] + precv[...].astype(jnp.float32)) * inv_root
    recip = lax.rsqrt(jnp.mean(values * values, axis=-1, keepdims=True) + EPS)
    normed = values * recip
    logits = jnp.dot(normed.astype(jnp.bfloat16), head_ref[...], preferred_element_type=jnp.float32)
    top = jnp.max(logits, axis=-1, keepdims=True)
    powers = jnp.exp(logits - top)
    total = jnp.sum(powers, axis=-1, keepdims=True)
    chosen = jnp.sum(logits * labels[...], axis=-1, keepdims=True)
    dlogits = (powers / total - labels[...]).astype(jnp.bfloat16)
    along = lax.dot_general(dlogits, head_ref[...], (((1,), (1,)), ((), ())),
                            preferred_element_type=jnp.float32)
    projected = jnp.mean(normed * along, axis=-1, keepdims=True)
    grad_values = ((along - normed * projected) * recip * inv_root).astype(jnp.bfloat16)
    gsend[0] = grad_values[:, :cols]
    g_out = remote(gsend.at[0], grecv, g_ss.at[0], g_rs.at[0], pair)
    g_out.start()
    gsend[1] = grad_values[:, cols:]
    gx_out = {}
    for j, peer in turns.items():
        gx_out[j] = remote(gsend.at[1], grad_x.at[j], gx_ss.at[j], gx_rs.at[j], peer)
        gx_out[j].start()
    loss = jnp.log(total) + top - chosen
    loss_ref[...] = jnp.transpose(jnp.broadcast_to(loss, (rows, 128)))[0:1, :]

    for k, of in enumerate((2, 1, -1, 0)):
        own[k] = tdot(tok[:, pl.ds(block(of), depth)], gsend[0]).astype(jnp.bfloat16)

    def summed(k, of):
        other = tdot(tok_y[:, pl.ds(block(of), depth)], grecv[...]).astype(jnp.bfloat16)
        return own[k].astype(jnp.float32) + other.astype(jnp.float32)

    def rounded(j, k):
        values = gsend[1] if j == 0 else grad_x[j]
        return tdot(tok_x[j, k], values).astype(jnp.bfloat16).astype(jnp.float32)

    def half_at(h):
        return pl.ds(h * half, half)

    def opp_copy(d):
        return remote(opp.at[half_at(d), :], opp_in.at[d], o_ss.at[d], o_rs.at[d], xs[d])

    def side_copy(d, h):
        return remote(sides.at[d, half_at(h), :], side_in.at[d, half_at(h), :],
                      s_ss.at[d, h], s_rs.at[d, h], xs[d])

    x_in[0].wait()
    x_in[1].wait()
    for k in range(2):
        terms[k] = rounded(0, k)
    g_out.wait_recv()
    opp[...] = summed(0, 2).astype(jnp.bfloat16)
    for d in range(2):
        opp_copy(d).start()
    for d in range(2):
        sides[d] = summed(1 + d, 1 - 2 * d).astype(jnp.bfloat16)
        side_copy(d, 1 - d).start()
    for i, j in enumerate(turns):
        x_out[2 * i].wait_recv()
        x_out[2 * i + 1].wait_recv()
        gx_out[j].wait_recv()
        terms[1] += rounded(j, 1)
    term_out[...] = terms[1].astype(jnp.bfloat16)
    r_out = remote(term_out, term_in, r_ss.at[0], r_rs.at[0], pair)
    r_out.start()
    for d in range(2):
        opp_copy(d).wait_recv()
        sides[d, half_at(d), :] = (sides[d, half_at(d), :].astype(jnp.float32)
                                   + opp_in[d].astype(jnp.float32)).astype(jnp.bfloat16)
        side_copy(d, d).start()
    for j in turns:
        terms[0] += rounded(j, 0)
    mine[0] = summed(3, 0)

    def mix_copy(q):
        return remote(mix_out.at[q], mix_in.at[q], m_ss.at[q], m_rs.at[q], me, ahead)

    def send_updated(q, grad):
        updated = wv[:, q * cols:(q + 1) * cols] - STEP * grad
        mix_out[q] = updated.astype(jnp.bfloat16)
        mix_copy(q).start()
        mine[q] = updated

    r_out.wait_recv()
    send_updated(1, terms[0] + term_in[...].astype(jnp.float32))
    for d in range(2):
        for h in range(2):
            side_copy(d, h).wait_recv()
    send_updated(0, mine[0] + side_in[0].astype(jnp.float32) + side_in[1].astype(jnp.float32))
    for q in (1, 0):
        mix_copy(q).wait_recv()
        mixed_ref[:, q * cols:(q + 1) * cols] = 0.5 * (mine[q] + mix_in[q].astype(jnp.float32))
    sent = tok_out + w_out[0] + w_out[1] + p_out + x_out + [g_out, r_out] + list(gx_out.values())
    for d in range(2):
        sent += [opp_copy(d), side_copy(d, 0), side_copy(d, 1)]
    for copy in sent + [mix_copy(0), mix_copy(1)]:
        copy.wait_send()


def step_call(level, tokens, weights, head, verdict):
    rows, wide = tokens.shape
    depth, kv = weights.shape
    grades = head.shape[1]
    cols = kv // SLABS
    any_spec = pl.BlockSpec(memory_space=pl.ANY)
    vmem = pl.BlockSpec(memory_space=pltpu.VMEM)
    bf16, f32 = jnp.bfloat16, jnp.float32
    sem = pltpu.SemaphoreType.DMA
    return pl.pallas_call(
        functools.partial(kernel, wide ** (-0.5), 1 << level),
        out_shape=(jax.ShapeDtypeStruct((depth, kv), f32), jax.ShapeDtypeStruct((1, rows), f32)),
        in_specs=[any_spec, any_spec, vmem, vmem],
        out_specs=(vmem, vmem),
        scratch_shapes=[
            pltpu.VMEM((rows, NX * depth), bf16), pltpu.VMEM((rows, NX * depth), bf16),
            pltpu.VMEM((depth, kv), f32), pltpu.VMEM((NX * depth, kv), bf16),
            pltpu.VMEM((rows, kv), f32), pltpu.VMEM((rows, grades), f32),
            pltpu.VMEM((rows, kv), bf16), pltpu.VMEM((rows, kv), bf16),
            pltpu.VMEM((SLABS, rows, cols), bf16), pltpu.VMEM((rows, cols), bf16),
            pltpu.VMEM((NX, depth, cols), bf16), pltpu.VMEM((SLABS, depth, cols), f32),
            pltpu.VMEM((depth, cols), bf16), pltpu.VMEM((2, depth, cols), bf16),
            pltpu.VMEM((2, depth // 2, cols), bf16), pltpu.VMEM((2, depth, cols), bf16),
            pltpu.VMEM((SLABS, depth, cols), bf16), pltpu.VMEM((SLABS, depth, cols), bf16),
            pltpu.VMEM((NX, 2, rows, depth), bf16), pltpu.VMEM((NX, rows, cols), bf16),
            pltpu.VMEM((2, depth, cols), f32), pltpu.VMEM((depth, cols), bf16),
            pltpu.VMEM((depth, cols), bf16),
            sem((4,)), sem((CHUNKS,)), sem((CHUNKS,)), sem((2, 3)), sem((2, 3)),
            sem((CHUNKS,)), sem((CHUNKS,)), sem((1,)), sem((1,)),
            sem((2,)), sem((2,)), sem((2, 2)), sem((2, 2)), sem((SLABS,)), sem((SLABS,)),
            sem((NX, 2)), sem((NX, 2)), sem((NX,)), sem((NX,)), sem((1,)), sem((1,)),
        ],
        compiler_params=pltpu.CompilerParams(collective_id=level, has_side_effects=True,
                                             vmem_limit_bytes=VMEM_BYTES),
        name="step",
    )(tokens, weights, head, verdict)


def local(tokens, weights, verdict_head, verdict, step_index):
    levels = lax.axis_size("rep").bit_length() - 1
    level = step_index[0] % levels
    mixed, loss = lax.switch(
        level, [functools.partial(step_call, lv) for lv in range(levels)],
        tokens, weights[0], verdict_head, verdict[None, :])
    return mixed[None], loss.reshape(-1)


def solution(mesh):
    return jax.shard_map(
        local,
        mesh=mesh,
        in_specs=(P(("rep", "fsdp"), None), P("rep", "fsdp", None), P(), P(("rep", "fsdp")), P()),
        out_specs=(P("rep", "fsdp", None), P(("rep", "fsdp"))),
        check_vma=False,
    )
```

```python
import functools

import jax
import jax.numpy as jnp
from jax import lax
from jax.experimental import pallas as pl
from jax.experimental.pallas import tpu as pltpu
from jax.sharding import PartitionSpec as P

MESH = pl.DeviceIdType.MESH
EPS = 1e-06
STEP = 8.0
NX = 4
CHUNKS = 4
SLABS = 2
VMEM_BYTES = 64000 << 10


def tdot(a, b):
    return lax.dot_general(a, b, (((0,), (0,)), ((), ())), preferred_element_type=jnp.float32)


def kernel(inv_root, distance, tok_hbm, w_hbm, head_ref, verdict_ref, mixed_ref, loss_ref,
           tok, tok_y, wv, wall, acc, labels, psend, precv, gsend, grecv, own, mine, opp, sides,
           opp_in, side_in, mix_out, mix_in, local_sem, tok_ss, tok_rs, w_ss, w_rs, p_ss, p_rs,
           g_ss, g_rs, o_ss, o_rs, s_ss, s_rs, m_ss, m_rs):
    rep, me = lax.axis_index("rep"), lax.axis_index("fsdp")
    row, x = me // NX, me % NX
    pair = (1 - row) * NX + x
    xs = [row * NX + (x + 1) % NX, row * NX + (x + NX - 1) % NX]
    depth, kv = wv.shape
    half = depth // 2
    rows = tok.shape[0]
    wide = NX * depth
    part = rows // CHUNKS

    n_rep = lax.axis_size("rep")
    ahead, behind = (rep + distance) % n_rep, (rep + n_rep - distance) % n_rep
    cols = kv // SLABS

    def remote(src, dst, ss, rs, peer, of_rep=None):
        return pltpu.make_async_remote_copy(src_ref=src, dst_ref=dst, send_sem=ss, recv_sem=rs,
                                            device_id=(rep if of_rep is None else of_rep, peer),
                                            device_id_type=MESH)

    def block(of):
        return pl.multiple_of(((x + of + NX) % NX) * depth, depth)

    w_in = pltpu.make_async_copy(w_hbm, wv, local_sem.at[0])
    w_in.start()
    t_in = pltpu.make_async_copy(tok_hbm.at[:, pl.ds(pl.multiple_of(row * wide, wide), wide)], tok,
                                 local_sem.at[1])
    t_in.start()
    barrier = pltpu.get_barrier_semaphore()
    for peer in xs + [pair]:
        pl.semaphore_signal(barrier, inc=1, device_id=(rep, peer), device_id_type=MESH)
    pl.semaphore_signal(barrier, inc=1, device_id=(behind, me), device_id_type=MESH)
    w_in.wait()
    wall[pl.ds(block(0), depth), :] = wv[...].astype(jnp.bfloat16)
    pl.semaphore_wait(barrier, 4)

    tok_out = []
    for c in range(CHUNKS):
        copy = remote(
            tok_hbm.at[pl.ds(c * part, part), pl.ds(pl.multiple_of((1 - row) * wide, wide), wide)],
            tok_y.at[pl.ds(c * part, part), :], tok_ss.at[c], tok_rs.at[c], pair)
        tok_out.append(copy)

    def w_copy(d, stage):
        hop = d if stage in (0, 2) else 1 - d
        of = 0 if stage < 2 else (-1 if d == 0 else 1)
        where = pl.ds(pl.multiple_of(block(of) + hop * half, half), half)
        return remote(wall.at[where, :], wall.at[where, :], w_ss.at[d, stage], w_rs.at[d, stage], xs[d])

    w_out = [[w_copy(d, s) for s in range(3)] for d in range(2)]
    for d in range(2):
        w_out[d][0].start()
    for copy in tok_out:
        copy.start()
    for d in range(2):
        w_out[d][1].start()

    hit = lax.broadcasted_iota(jnp.int32, (labels.shape[1], rows), 0) == verdict_ref[...]
    labels[...] = jnp.transpose(hit.astype(jnp.float32))
    t_in.wait()

    def product(of):
        return jnp.dot(tok[:, pl.ds(block(of), depth)], wall[pl.ds(block(of), depth), :],
                       preferred_element_type=jnp.float32)

    acc[...] = product(0)
    for d in range(2):
        w_out[d][0].wait_recv()
        w_out[d][2].start()
    for d in range(2):
        w_out[d][1].wait_recv()
    acc[...] += product(-1) + product(1)
    for d in range(2):
        w_out[d][2].wait_recv()
    acc[...] += product(2)

    p_out = []
    for c in range(CHUNKS):
        here = pl.ds(c * part, part)
        tok_out[c].wait_recv()
        psend[here, :] = jnp.dot(tok_y[here, :], wall[...],
                                 preferred_element_type=jnp.float32).astype(jnp.bfloat16)
        copy = remote(psend.at[here, :], precv.at[here, :], p_ss.at[c], p_rs.at[c], pair)
        copy.start()
        p_out.append(copy)
    for copy in p_out:
        copy.wait_recv()

    values = (acc[...] + precv[...].astype(jnp.float32)) * inv_root
    recip = lax.rsqrt(jnp.mean(values * values, axis=-1, keepdims=True) + EPS)
    normed = values * recip
    logits = jnp.dot(normed.astype(jnp.bfloat16), head_ref[...], preferred_element_type=jnp.float32)
    top = jnp.max(logits, axis=-1, keepdims=True)
    powers = jnp.exp(logits - top)
    total = jnp.sum(powers, axis=-1, keepdims=True)
    chosen = jnp.sum(logits * labels[...], axis=-1, keepdims=True)
    dlogits = (powers / total - labels[...]).astype(jnp.bfloat16)
    along = lax.dot_general(dlogits, head_ref[...], (((1,), (1,)), ((), ())),
                            preferred_element_type=jnp.float32)
    projected = jnp.mean(normed * along, axis=-1, keepdims=True)
    grad_values = ((along - normed * projected) * recip * inv_root).astype(jnp.bfloat16)
    g_out = []
    for q in range(SLABS):
        gsend[q] = grad_values[:, q * cols:(q + 1) * cols]
        copy = remote(gsend.at[q], grecv.at[q], g_ss.at[q], g_rs.at[q], pair)
        copy.start()
        g_out.append(copy)
    loss = jnp.log(total) + top - chosen
    loss_ref[...] = jnp.transpose(jnp.broadcast_to(loss, (rows, 128)))[0:1, :]

    for q in range(SLABS):
        for k, of in enumerate((2, 1, -1, 0)):
            own[q, k] = tdot(tok[:, pl.ds(block(of), depth)], gsend[q]).astype(jnp.bfloat16)

    def summed(q, k, of):
        other = tdot(tok_y[:, pl.ds(block(of), depth)], grecv[q]).astype(jnp.bfloat16)
        return own[q, k].astype(jnp.float32) + other.astype(jnp.float32)

    def half_at(h):
        return pl.ds(h * half, half)

    def opp_copy(q, d):
        return remote(opp.at[q, half_at(d), :], opp_in.at[q, d], o_ss.at[q, d], o_rs.at[q, d], xs[d])

    def side_copy(q, d, h):
        return remote(sides.at[q, d, half_at(h), :], side_in.at[q, d, half_at(h), :],
                      s_ss.at[q, d, h], s_rs.at[q, d, h], xs[d])

    def add_opposite(q):
        g_out[q].wait_recv()
        opp[q] = summed(q, 0, 2).astype(jnp.bfloat16)

    def send_opposite(q):
        for d in range(2):
            opp_copy(q, d).start()

    def send_plain(q):
        for d in range(2):
            sides[q, d] = summed(q, 1 + d, 1 - 2 * d).astype(jnp.bfloat16)
            side_copy(q, d, 1 - d).start()

    def send_added(q):
        for d in range(2):
            opp_copy(q, d).wait_recv()
            sides[q, d, half_at(d), :] = (sides[q, d, half_at(d), :].astype(jnp.float32)
                                          + opp_in[q, d].astype(jnp.float32)).astype(jnp.bfloat16)
            side_copy(q, d, d).start()

    def mix_copy(q, h):
        return remote(mix_out.at[q, half_at(h), :], mix_in.at[q, half_at(h), :],
                      m_ss.at[q, h], m_rs.at[q, h], me, ahead)

    def send_updated(q):
        for h in range(2):
            for d in range(2):
                side_copy(q, d, h).wait_recv()
            grad = (mine[q, half_at(h), :] + side_in[q, 0, half_at(h), :].astype(jnp.float32)
                    + side_in[q, 1, half_at(h), :].astype(jnp.float32))
            updated = wv[half_at(h), q * cols:(q + 1) * cols] - STEP * grad
            mix_out[q, half_at(h), :] = updated.astype(jnp.bfloat16)
            mix_copy(q, h).start()
            mine[q, half_at(h), :] = updated

    add_opposite(0)
    for q in range(SLABS):
        send_opposite(q)
        send_plain(q)
        if q + 1 < SLABS:
            add_opposite(q + 1)
        else:
            for p in range(SLABS):
                mine[p] = summed(p, 3, 0)
            for p in range(q):
                send_updated(p)
        send_added(q)
    send_updated(SLABS - 1)
    for q in range(SLABS):
        for h in range(2):
            mix_copy(q, h).wait_recv()
            mixed_ref[half_at(h), q * cols:(q + 1) * cols] = 0.5 * (
                mine[q, half_at(h), :] + mix_in[q, half_at(h), :].astype(jnp.float32))
    for copy in tok_out + w_out[0] + w_out[1] + p_out + g_out:
        copy.wait_send()
    for q in range(SLABS):
        for d in range(2):
            opp_copy(q, d).wait_send()
            mix_copy(q, d).wait_send()
            for h in range(2):
                side_copy(q, d, h).wait_send()


def step_call(level, tokens, weights, head, verdict):
    rows, wide = tokens.shape
    depth, kv = weights.shape
    grades = head.shape[1]
    cols = kv // SLABS
    any_spec = pl.BlockSpec(memory_space=pl.ANY)
    vmem = pl.BlockSpec(memory_space=pltpu.VMEM)
    bf16, f32 = jnp.bfloat16, jnp.float32
    sem = pltpu.SemaphoreType.DMA
    return pl.pallas_call(
        functools.partial(kernel, wide ** (-0.5), 1 << level),
        out_shape=(jax.ShapeDtypeStruct((depth, kv), f32), jax.ShapeDtypeStruct((1, rows), f32)),
        in_specs=[any_spec, any_spec, vmem, vmem],
        out_specs=(vmem, vmem),
        scratch_shapes=[
            pltpu.VMEM((rows, NX * depth), bf16), pltpu.VMEM((rows, NX * depth), bf16),
            pltpu.VMEM((depth, kv), f32), pltpu.VMEM((NX * depth, kv), bf16),
            pltpu.VMEM((rows, kv), f32), pltpu.VMEM((rows, grades), f32),
            pltpu.VMEM((rows, kv), bf16), pltpu.VMEM((rows, kv), bf16),
            pltpu.VMEM((SLABS, rows, cols), bf16), pltpu.VMEM((SLABS, rows, cols), bf16),
            pltpu.VMEM((SLABS, NX, depth, cols), bf16), pltpu.VMEM((SLABS, depth, cols), f32),
            pltpu.VMEM((SLABS, depth, cols), bf16), pltpu.VMEM((SLABS, 2, depth, cols), bf16),
            pltpu.VMEM((SLABS, 2, depth // 2, cols), bf16), pltpu.VMEM((SLABS, 2, depth, cols), bf16),
            pltpu.VMEM((SLABS, depth, cols), bf16), pltpu.VMEM((SLABS, depth, cols), bf16),
            sem((2,)), sem((CHUNKS,)), sem((CHUNKS,)), sem((2, 3)), sem((2, 3)),
            sem((CHUNKS,)), sem((CHUNKS,)), sem((SLABS,)), sem((SLABS,)),
            sem((SLABS, 2)), sem((SLABS, 2)), sem((SLABS, 2, 2)), sem((SLABS, 2, 2)),
            sem((SLABS, 2)), sem((SLABS, 2)),
        ],
        compiler_params=pltpu.CompilerParams(collective_id=level, has_side_effects=True,
                                             vmem_limit_bytes=VMEM_BYTES),
        name="step",
    )(tokens, weights, head, verdict)


def local(tokens, weights, verdict_head, verdict, step_index):
    levels = lax.axis_size("rep").bit_length() - 1
    level = step_index[0] % levels
    mixed, loss = lax.switch(
        level, [functools.partial(step_call, lv) for lv in range(levels)],
        tokens, weights[0], verdict_head, verdict[None, :])
    return mixed[None], loss.reshape(-1)


def solution(mesh):
    return jax.shard_map(
        local,
        mesh=mesh,
        in_specs=(P(("rep", "fsdp"), None), P("rep", "fsdp", None), P(), P(("rep", "fsdp")), P()),
        out_specs=(P("rep", "fsdp", None), P(("rep", "fsdp"))),
        check_vma=False,
    )
```
